32 devices in a mesh: row: 16 (over z, y, core), col: 2 (over x).
Axes of the slice: x: 2, y: 2, z: 4, core: 2. Of those that a mesh axis runs over, the one named last changes fastest.
Arguments:
- samples: float32 [256, 16384], P(None, 'col'), may hold values from -0.8 to 0.8
- values: float32 [16384, 16384], P('row', 'col'), may hold values from -6 to 6
- diag_entries: float32 [16384], P('row'), may hold values from 16 to 32
- block_mask: int32 [64, 64], replicated, may hold values 0 or 1
Outputs:
- updated: float32 [16384, 16384], P('row', 'col')
The draws below stay inside these ranges and needn't reach their ends.
All inputs are finite; a program needn't handle non-finite values.
Results may differ from the reference program's by a relative error of at most 0.0003.
Values sent between devices are 32-bit elements; how exact they have to be, the bound alone decides.
A program may use at most 192 MiB of HBM per device.

```python
import math
import jax
import jax.numpy as jnp
from jax import lax

P_SIZE = 16384
BLOCKS = 64
SAMPLES = 256


def set_ends(entries, key, low, largest):
    longest = entries.shape.index(max(entries.shape))
    spots = []
    for shift in (0, 1):
        where = [jax.random.randint(jax.random.fold_in(key, axis), (), 0, length) for axis, length in enumerate(entries.shape)]
        where[longest] = (where[longest] + shift) % entries.shape[longest]
        spots.append(tuple(where))
    return entries.at[spots[0]].set(low).at[spots[1]].set(largest)


def spiked(result, key, source, target, parts, factor):
    owner, partner = [(jnp.arange(result.shape[dim]) // (result.shape[dim] // parts)).reshape([-1 if axis == dim else 1 for axis in range(result.ndim)]) for dim in (source, target)]
    chosen = jax.random.permutation(key, parts)[partner]
    strong = (owner == chosen) | (owner == (partner + parts // 2) % parts)
    return jnp.where(strong, factor * result, result)


def steps_of(stream_key, dims, shards, low, high):
    loudness, own = 1.0, jax.random.fold_in(stream_key, 6)
    for axis_at, shards_of in shards:
        heights = jnp.exp(jax.random.uniform(jax.random.fold_in(own, axis_at), (shards_of,), jnp.float32, low / len(shards), high / len(shards)))
        loudness = loudness * jnp.repeat(heights, dims[axis_at] // shards_of).reshape([-1 if axis == axis_at else 1 for axis in range(len(dims))])
    return loudness


def centred(key, extent, spread, most, cuts=(), held_as=jnp.bfloat16):
    values = jax.random.normal(key, extent, jnp.float32) * spread
    if len(cuts) > 0:
        values = steps_of(key, extent, cuts, -0.22, 0.18) * values
    return jnp.clip(values, min=-most, max=most).astype(held_as)


def noise_with(stream_key, shape, spread, reach, pieces, heavy, held_as=jnp.bfloat16):
    values = spread * jax.random.normal(stream_key, shape, jnp.float32)
    if pieces:
        values = values * steps_of(stream_key, shape, pieces, -0.22, 0.18)
    return jnp.clip(spiked(values, jax.random.fold_in(stream_key, 3), *heavy), -reach, reach).astype(held_as)


def setup_inputs(seed: int = 0) -> dict:
    keys = jax.random.split(jax.random.key(seed), 5)
    samples = noise_with(keys[0], (SAMPLES, P_SIZE), 0.13, 0.8, ((1, 2),), (1, 0, 2, 2.0), jnp.float32)
    values = centred(keys[1], (P_SIZE, P_SIZE), 1.0, 6.0, ((0, 16), (1, 2)), jnp.float32)
    diag_entries = jnp.clip(jnp.exp(math.log(32.0) - 0.6931472 * jax.random.uniform(keys[2], (P_SIZE,), jnp.float32) ** steps_of(keys[2], (P_SIZE,), ((0, 16),), -0.2, 0.2)), 16.0, 32.0)
    block_mask = set_ends((jax.random.randint(keys[3], (BLOCKS, BLOCKS), 0, 2) < 1).astype(jnp.int32), jax.random.fold_in(keys[3], 1), 0, 1)
    return dict(samples=samples, values=values, diag_entries=diag_entries, block_mask=block_mask)


step_size = 8.0
penalty = 0.05


def reference(samples, values, diag_entries, block_mask):
    order_total = values.shape[0]
    mask_block = order_total // BLOCKS
    dense_mask = jnp.repeat(jnp.repeat(block_mask, mask_block, axis=0), mask_block, axis=1).astype(jnp.float32)
    indices = jnp.arange(order_total, dtype=jnp.int32)
    on_diag = indices[:, None] == indices[None, :]
    omega = jnp.where(on_diag, diag_entries[:, None], dense_mask * values)
    projected = jnp.dot(samples, omega, precision=lax.Precision.HIGHEST, preferred_element_type=jnp.float32)
    sample_count = samples.shape[0]
    row_block = order_total // BLOCKS

    def update_rows(block_index):
        begin = (block_index * row_block).astype(jnp.int32)
        x_rows = lax.dynamic_slice_in_dim(samples, begin, row_block, 1)
        y_rows = lax.dynamic_slice_in_dim(projected, begin, row_block, 1)
        w_rows = lax.dot_general(x_rows, projected, (((0,), (0,)), ((), ())), precision=lax.Precision.HIGHEST, preferred_element_type=jnp.float32)
        wt_rows = lax.dot_general(y_rows, samples, (((0,), (0,)), ((), ())), precision=lax.Precision.HIGHEST, preferred_element_type=jnp.float32)
        gradient = 0.5 * (w_rows / sample_count + wt_rows / sample_count)
        row_ids = begin + jnp.arange(row_block, dtype=jnp.int32)
        diag_here = row_ids[:, None] == indices[None, :]
        diag_rows = lax.dynamic_slice_in_dim(diag_entries, begin, row_block, 0)
        gradient = gradient - jnp.where(diag_here, 1.0 / diag_rows[:, None], jnp.float32(0.0))
        omega_rows = lax.dynamic_slice_in_dim(omega, begin, row_block, 0)
        stepped = omega_rows - step_size * gradient
        shrunk = jnp.sign(stepped) * jnp.maximum(jnp.abs(stepped) - step_size * penalty, jnp.float32(0.0))
        return jnp.where(diag_here, stepped, shrunk)

    blocks_out = lax.map(update_rows, jnp.arange(BLOCKS, dtype=jnp.int32))
    return blocks_out.reshape(order_total, order_total)
```

```python
import functools

import jax
import jax.numpy as jnp
from jax import lax
from jax.experimental import pallas as pl
from jax.experimental.pallas import tpu as pltpu
from jax.sharding import PartitionSpec as P

step_size = 8.0
penalty = 0.05
MESH = pl.DeviceIdType.MESH
VM = pltpu.VMEM
LIMIT = 60 * 1024 * 1024


def split(x):
    high = x.astype(jnp.bfloat16)
    low = (x - high.astype(jnp.float32)).astype(jnp.bfloat16)
    return high, low


def dot(a, b):
    return jnp.dot(a, b, preferred_element_type=jnp.float32)


def fetch_kernel(groups, per_group, samples_ref, out_ref, local_sem, send_sem, recv_sem):
    row, col = lax.axis_index("row"), lax.axis_index("col")
    owner = row // per_group
    width = out_ref.shape[1]
    at = pl.multiple_of(row % per_group * width, width)
    source = samples_ref.at[:, pl.ds(at, width)]
    barrier = pltpu.get_barrier_semaphore()
    for shift in range(1, groups):
        pl.semaphore_signal(
            barrier, inc=1, device_id=(row, lax.rem(col + shift, groups)), device_id_type=MESH
        )
    pl.semaphore_wait(barrier, groups - 1)

    def remote(shift):
        return pltpu.make_async_remote_copy(
            src_ref=source,
            dst_ref=out_ref,
            send_sem=send_sem.at[shift],
            recv_sem=recv_sem,
            device_id=(row, lax.rem(col + shift, groups)),
            device_id_type=MESH,
        )

    @pl.when(col == owner)
    def _():
        for shift in range(1, groups):
            remote(shift).start()
        own = pltpu.make_async_copy(source, out_ref, local_sem)
        own.start()
        own.wait()
        for shift in range(1, groups):
            remote(shift).wait_send()

    @pl.when(col != owner)
    def _():
        remote(1).wait_recv()


def project_kernel(offset_ref, rows_ref, values_ref, diag_ref, mask_ref, out_ref, high_ref, low_ref):
    step = pl.program_id(0)
    tile = values_ref.shape[1]
    parts = mask_ref.shape[0]
    height = values_ref.shape[0] // parts

    @pl.when(step == 0)
    def _():
        high_ref[...], low_ref[...] = split(rows_ref[...])

    total = None
    for part in range(parts):
        begin = part * height
        rows = pl.ds(begin, height)
        omega = omega_tile(offset_ref, values_ref, diag_ref, mask_ref, step, part)
        high, low = split(omega)
        left = high_ref[:, rows]
        term = dot(left, high) + dot(low_ref[:, rows], high) + dot(left, low)
        total = term if total is None else total + term
    out_ref[...] = total


def on_diagonal(offset_ref, step, begin, shape):
    rows = lax.broadcasted_iota(jnp.int32, shape, 0) + (offset_ref[0] + begin)
    cols = lax.broadcasted_iota(jnp.int32, shape, 1) + (offset_ref[1] + step * shape[1])
    return rows == cols


def omega_tile(offset_ref, values_ref, diag_ref, mask_ref, step, part):
    height = values_ref.shape[0] // mask_ref.shape[0]
    rows = pl.ds(part * height, height)
    masked = values_ref[rows, :] * mask_ref[part : part + 1, :]
    diagonal = on_diagonal(offset_ref, step, part * height, masked.shape)
    return jnp.where(diagonal, diag_ref[rows, :], masked)


def update_kernel(
    offset_ref, left_ref, proj_ref, samples_ref, values_ref, diag_ref, mask_ref, out_ref, left_high, left_low, high_ref, low_ref
):
    step = pl.program_id(0)
    count = samples_ref.shape[0]
    parts = mask_ref.shape[0]
    height = values_ref.shape[0] // parts

    @pl.when(step == 0)
    def _():
        left_high[...], left_low[...] = split(left_ref[...])

    high_ref[:count, :], low_ref[:count, :] = split(proj_ref[...])
    high_ref[count:, :], low_ref[count:, :] = split(samples_ref[...])
    for part in range(parts):
        rows = pl.ds(part * height, height)
        cross = (
            dot(left_high[rows, :], high_ref[...])
            + dot(left_low[rows, :], high_ref[...])
            + dot(left_high[rows, :], low_ref[...])
        )
        diagonal = on_diagonal(offset_ref, step, part * height, cross.shape)
        diag = diag_ref[rows, :]
        omega = jnp.where(diagonal, diag, values_ref[rows, :] * mask_ref[part : part + 1, :])
        stepped = omega - cross * (0.5 * step_size / count)
        limit = step_size * penalty
        shrunk = stepped - jnp.clip(stepped, -limit, limit)
        out_ref[rows, :] = jnp.where(diagonal, stepped + step_size / diag, shrunk)


def reduce_kernel(lines, groups, per_group, chunks, part_ref, out_ref, proj_ref, *scratch):
    (core_in, y_in, a_right, a_left, b_right, b_left, y_right, y_left) = scratch[:8]
    send, recv = scratch[8], scratch[9]
    row, col = lax.axis_index("row"), lax.axis_index("col")
    core, side, line = row % 2, row // 2 % 2, row // 4
    last = lines - 1
    core_mate = row + 1 - 2 * core
    y_mate = row + 2 - 4 * side
    up, down = row + 4, row - 4
    samples, order = part_ref.shape
    deep = samples // chunks
    half, quarter, eighth, sixteenth = order // 2, order // 4, order // 8, order // 16
    has_up, has_down = line < last, line > 0
    owner = row // per_group
    width = proj_ref.shape[1]
    slice_at = pl.multiple_of(row % per_group * width, width)

    barrier = pltpu.get_barrier_semaphore()

    def greet(target):
        pl.semaphore_signal(barrier, inc=1, device_id=target, device_id_type=MESH)

    greet((core_mate, col))
    greet((y_mate, col))
    pl.when(has_up)(lambda: greet((up, col)))
    pl.when(has_down)(lambda: greet((down, col)))
    for shift in range(1, groups):
        greet((row, lax.rem(col + shift, groups)))
    ends = jnp.where(has_up, 1, 0) + jnp.where(has_down, 1, 0)
    pl.semaphore_wait(barrier, 2 + groups - 1 + ends)

    def span(at, size):
        return pl.ds(pl.multiple_of(at, sixteenth), size)

    def rows_of(q):
        return pl.ds(pl.multiple_of(q * deep, deep), deep)

    def a_at(k, v):
        return k * half + v * eighth

    def b_at(k):
        return k * half + quarter

    def copy(kind, q, source, target, device, landing=None):
        return pltpu.make_async_remote_copy(
            src_ref=source,
            dst_ref=target,
            send_sem=send.at[kind, q],
            recv_sem=recv.at[kind if landing is None else landing, q],
            device_id=device,
            device_id_type=MESH,
        )

    def whole(ref, q):
        return ref.at[rows_of(q), :]

    def out_at(q, at, size):
        return out_ref.at[rows_of(q), span(at, size)]

    def c_core(q):
        return copy(0, q, part_ref.at[rows_of(q), span((1 - core) * half, half)], whole(core_in, q), (core_mate, col))

    def c_y(q):
        return copy(1, q, core_in.at[rows_of(q), span((1 - side) * eighth, eighth)], whole(y_in, q), (y_mate, col))

    def c_b_right(q, first):
        source = core_in.at[rows_of(q), span(quarter, eighth)] if first else whole(b_right, q)
        return copy(2, q, source, whole(b_right, q), (up, col))

    def c_b_left(q, first):
        source = core_in.at[rows_of(q), span(quarter + eighth, eighth)] if first else whole(b_left, q)
        return copy(3, q, source, whole(b_left, q), (down, col))

    def c_a_right(q, first):
        source = y_in.at[rows_of(q), span(0, sixteenth)] if first else whole(a_right, q)
        return copy(4, q, source, whole(a_right, q), (up, col))

    def c_a_left(q, first):
        source = y_in.at[rows_of(q), span(sixteenth, sixteenth)] if first else whole(a_left, q)
        return copy(5, q, source, whole(a_left, q), (down, col))

    def c_y_right(q):
        return copy(6, q, whole(b_right, q), whole(y_right, q), (y_mate, col))

    def c_y_left(q):
        return copy(7, q, whole(b_left, q), whole(y_left, q), (y_mate, col))

    def spread(kind, q, at, size, target):
        return copy(kind, q, out_at(q, at, size), out_at(q, at, size), (target, col))

    def b_piece(flow):
        return b_at(core) + flow * eighth, eighth

    def a_piece(flow, v):
        return a_at(core, v) + flow * sixteenth, sixteenth

    def c_b_back(q, flow):
        return spread(8 + flow, q, *b_piece(flow), (down, up)[flow])

    def c_a_back(q, flow):
        return spread(10 + flow, q, *a_piece(flow, side), (down, up)[flow])

    def c_y_back(q, flow):
        return spread(12 + flow, q, *a_piece(flow, side), y_mate)

    def y_back_arrival(q, flow):
        return spread(12 + flow, q, *a_piece(flow, 1 - side), y_mate)

    def c_core_back(q, index, at, size):
        return copy(14 + index, q, out_at(q, at, size), out_at(q, at, size), (core_mate, col), 14 + index)

    def core_arrival(q, index, at, size):
        other = at - core * half + (1 - core) * half
        return c_core_back(q, index, other, size)

    pieces = []
    for flow in range(2):
        pieces += [(flow, *b_piece(flow)), (2 + flow, *a_piece(flow, side)), (4 + flow, *a_piece(flow, 1 - side))]

    def core_pieces_in(q):
        for flow in range(2):
            core_arrival(q, flow, *b_piece(flow)).wait_recv()
            for index, v in ((2, side), (4, 1 - side)):
                core_arrival(q, index + flow, *a_piece(flow, v)).wait_recv()

    def c_proj(q, shift):
        return copy(
            20 + shift,
            q,
            out_ref.at[rows_of(q), pl.ds(slice_at, width)],
            whole(proj_ref, q),
            (row, lax.rem(col + shift, groups)),
            21,
        )

    def at_stage(t, offset, condition, action):
        q = t - offset
        live = jnp.logical_and(q >= 0, q < chunks)
        if condition is not None:
            live = jnp.logical_and(live, condition)
        pl.when(live)(lambda: action(jnp.clip(q, 0, chunks - 1)))

    def begin(q):
        c_core(q).wait_recv()
        rows = rows_of(q)
        core_in[rows, :] = core_in[rows, :] + part_ref[rows, span(core * half, half)]
        c_y(q).start()
        pl.when(line == 0)(lambda: c_b_right(q, True).start())
        pl.when(line == last)(lambda: c_b_left(q, True).start())

    def after_y(q):
        c_y(q).wait_recv()
        rows = rows_of(q)
        y_in[rows, :] = y_in[rows, :] + core_in[rows, span(side * eighth, eighth)]
        pl.when(line == 0)(lambda: c_a_right(q, True).start())
        pl.when(line == last)(lambda: c_a_left(q, True).start())

    def b_hop(q, flow):
        ref, make = (b_right, c_b_right) if flow == 0 else (b_left, c_b_left)
        make(q, False).wait_recv()
        rows = rows_of(q)
        ref[rows, :] = ref[rows, :] + core_in[rows, span(quarter + flow * eighth, eighth)]
        going = has_up if flow == 0 else has_down
        pl.when(going)(lambda: make(q, False).start())
        pl.when(jnp.logical_not(going))(lambda: (c_y_right if flow == 0 else c_y_left)(q).start())

    def done_a(q, flow, forward):
        pl.when(forward)(lambda: c_a_back(q, flow).start())
        c_y_back(q, flow).start()
        c_core_back(q, 2 + flow, *a_piece(flow, side)).start()

    def done_b(q, flow, forward):
        pl.when(forward)(lambda: c_b_back(q, flow).start())
        c_core_back(q, flow, *b_piece(flow)).start()

    def a_hop(q, flow):
        ref, make = (a_right, c_a_right) if flow == 0 else (a_left, c_a_left)
        make(q, False).wait_recv()
        rows = rows_of(q)
        value = ref[rows, :] + y_in[rows, span(flow * sixteenth, sixteenth)]
        going = has_up if flow == 0 else has_down

        @pl.when(going)
        def _():
            ref[rows, :] = value
            make(q, False).start()

        @pl.when(jnp.logical_not(going))
        def _():
            out_ref[rows, span(*a_piece(flow, side))] = value
            done_a(q, flow, True)

    def b_end(q, flow):
        ref, other, make = (b_right, y_right, c_y_right) if flow == 0 else (b_left, y_left, c_y_left)
        make(q).wait_recv()
        rows = rows_of(q)
        out_ref[rows, span(*b_piece(flow))] = ref[rows, :] + other[rows, :]
        done_b(q, flow, True)

    def back(q, flow):
        forward = has_down if flow == 0 else has_up
        c_a_back(q, flow).wait_recv()
        done_a(q, flow, forward)
        c_b_back(q, flow).wait_recv()
        done_b(q, flow, forward)

    def y_gather(q, flow):
        y_back_arrival(q, flow).wait_recv()
        c_core_back(q, 4 + flow, *a_piece(flow, 1 - side)).start()

    def finish(q):
        core_pieces_in(q)
        rows = rows_of(q)

        @pl.when(col == owner)
        def _():
            for shift in range(1, groups):
                c_proj(q, shift).start()
            proj_ref[rows, :] = out_ref[rows, pl.ds(slice_at, width)]

    @pl.loop(0, chunks)
    def _(q):
        c_core(q).start()

    total = 2 * lines + 2

    @pl.loop(0, chunks + total)
    def _(t):
        at_stage(t, 0, None, begin)
        at_stage(t, 1, None, after_y)
        at_stage(t, line, has_down, lambda q: b_hop(q, 0))
        at_stage(t, last - line, has_up, lambda q: b_hop(q, 1))
        at_stage(t, 1 + line, has_down, lambda q: a_hop(q, 0))
        at_stage(t, lines - line, has_up, lambda q: a_hop(q, 1))
        at_stage(t, lines, line == last, lambda q: b_end(q, 0))
        at_stage(t, lines, line == 0, lambda q: b_end(q, 1))
        at_stage(t, lines + last - line, has_up, lambda q: back(q, 0))
        at_stage(t, lines + line, has_down, lambda q: back(q, 1))
        at_stage(t, lines + last - line + 1, None, lambda q: y_gather(q, 0))
        at_stage(t, lines + line + 1, None, lambda q: y_gather(q, 1))
        at_stage(t, 2 * lines + 1, None, finish)

    @pl.loop(0, chunks)
    def _(q):
        c_core(q).wait_send()
        c_y(q).wait_send()
        pl.when(has_up)(lambda: c_b_right(q, False).wait_send())
        pl.when(has_down)(lambda: c_b_left(q, False).wait_send())
        pl.when(has_up)(lambda: c_a_right(q, False).wait_send())
        pl.when(has_down)(lambda: c_a_left(q, False).wait_send())
        pl.when(line == last)(lambda: c_y_right(q).wait_send())
        pl.when(line == 0)(lambda: c_y_left(q).wait_send())
        for flow, forward in ((0, has_down), (1, has_up)):
            pl.when(forward)(lambda flow=flow: c_b_back(q, flow).wait_send())
            pl.when(forward)(lambda flow=flow: c_a_back(q, flow).wait_send())
            c_y_back(q, flow).wait_send()
        for index, at, size in pieces:
            c_core_back(q, index, at, size).wait_send()

        @pl.when(col == owner)
        def _():
            for shift in range(1, groups):
                c_proj(q, shift).wait_send()

        @pl.when(col != owner)
        def _():
            c_proj(q, 1).wait_recv()


def per_device(samples, values, diag_entries, block_mask):
    height, order = values.shape
    count = samples.shape[0]
    groups = lax.axis_size("col")
    lines = lax.axis_size("row") // 4
    per_group = order // height
    row_at = lax.axis_index("row") * height
    col_at = lax.axis_index("col") * order
    block = groups * order // block_mask.shape[0]
    tile_mask = lax.dynamic_slice(
        block_mask, (row_at // block, col_at // block), (height // block, order // block)
    )
    mask = jnp.repeat(tile_mask.astype(jnp.float32), block, axis=1)
    diag = diag_entries[:, None]
    offsets = jnp.stack([row_at, col_at]).astype(jnp.int32)
    anywhere = pl.BlockSpec(memory_space=pl.ANY)
    in_vmem = pl.BlockSpec(memory_space=VM)
    row_samples = pl.pallas_call(
        functools.partial(fetch_kernel, groups, per_group),
        out_shape=jax.ShapeDtypeStruct((count, height), jnp.float32),
        in_specs=[anywhere],
        out_specs=in_vmem,
        scratch_shapes=[
            pltpu.SemaphoreType.DMA,
            pltpu.SemaphoreType.DMA((groups,)),
            pltpu.SemaphoreType.DMA,
        ],
        compiler_params=pltpu.CompilerParams(collective_id=0, has_side_effects=True),
    )(samples)

    tile = 2 * block
    grid = order // tile
    fixed = lambda shape: pl.BlockSpec(shape, lambda i, s: (0, 0))
    moving = lambda rows: pl.BlockSpec((rows, tile), lambda i, s: (0, i))
    parts = mask.shape[0]
    partial_value = pl.pallas_call(
        project_kernel,
        out_shape=jax.ShapeDtypeStruct((count, order), jnp.float32),
        grid_spec=pltpu.PrefetchScalarGridSpec(
            num_scalar_prefetch=1,
            grid=(grid,),
            in_specs=[fixed((count, height)), moving(height), fixed((height, 1)), moving(parts)],
            out_specs=moving(count),
            scratch_shapes=[VM((count, height), jnp.bfloat16)] * 2,
        ),
        compiler_params=pltpu.CompilerParams(dimension_semantics=("arbitrary",), vmem_limit_bytes=LIMIT),
    )(offsets, row_samples, values, diag, mask)

    chunks = max(1, min(8, count // 8))
    eighth, sixteenth = order // 8, order // 16
    widths = [order // 2, eighth, sixteenth, sixteenth, eighth, eighth, eighth, eighth]
    kinds = 21 + groups
    projected, row_proj = pl.pallas_call(
        functools.partial(reduce_kernel, lines, groups, per_group, chunks),
        out_shape=(
            jax.ShapeDtypeStruct((count, order), jnp.float32),
            jax.ShapeDtypeStruct((count, height), jnp.float32),
        ),
        in_specs=[in_vmem],
        out_specs=(in_vmem, in_vmem),
        scratch_shapes=[VM((count, w), jnp.float32) for w in widths]
        + [pltpu.SemaphoreType.DMA((kinds, chunks)), pltpu.SemaphoreType.DMA((kinds, chunks))],
        compiler_params=pltpu.CompilerParams(
            collective_id=1, has_side_effects=True, vmem_limit_bytes=LIMIT
        ),
    )(partial_value)

    left = jnp.concatenate([row_samples, row_proj], axis=0).T
    return pl.pallas_call(
        update_kernel,
        out_shape=jax.ShapeDtypeStruct((height, order), jnp.float32),
        grid_spec=pltpu.PrefetchScalarGridSpec(
            num_scalar_prefetch=1,
            grid=(grid,),
            in_specs=[
                fixed((height, 2 * count)),
                moving(count),
                moving(count),
                moving(height),
                fixed((height, 1)),
                moving(parts),
            ],
            out_specs=moving(height),
            scratch_shapes=[VM((height, 2 * count), jnp.bfloat16)] * 2
            + [VM((2 * count, tile), jnp.bfloat16)] * 2,
        ),
        compiler_params=pltpu.CompilerParams(dimension_semantics=("arbitrary",), vmem_limit_bytes=LIMIT),
    )(offsets, left, projected, samples, values, diag, mask)


def solution(mesh):
    in_specs = (P(None, "col"), P("row", "col"), P("row"), P())
    out_specs = P("row", "col")
    return jax.shard_map(
        per_device, mesh=mesh, in_specs=in_specs, out_specs=out_specs, check_vma=False
    )
```

```python
import functools

import jax
import jax.numpy as jnp
from jax import lax
from jax.experimental import pallas as pl
from jax.experimental.pallas import tpu as pltpu
from jax.sharding import PartitionSpec as P

step_size = 8.0
penalty = 0.05
MESH = pl.DeviceIdType.MESH
VM = pltpu.VMEM
LIMIT = 60 * 1024 * 1024


def split(x):
    high = x.astype(jnp.bfloat16)
    low = (x - high.astype(jnp.float32)).astype(jnp.bfloat16)
    return high, low


def dot(a, b):
    return jnp.dot(a, b, preferred_element_type=jnp.float32)


def on_diagonal(row_at, col_at, shape):
    rows = lax.broadcasted_iota(jnp.int32, shape, 0) + row_at
    cols = lax.broadcasted_iota(jnp.int32, shape, 1) + col_at
    return rows == cols


def crosses(row_at, col_at, shape):
    return jnp.logical_and(row_at < col_at + shape[1], col_at < row_at + shape[0])


def update_kernel(
    offset_ref, left_ref, proj_ref, samples_ref, values_ref, diag_ref, mask_ref, out_ref, lefts, rights
):
    step = pl.program_id(0)
    count = samples_ref.shape[0]
    parts = mask_ref.shape[0]
    height = values_ref.shape[0] // parts
    tile = values_ref.shape[1]
    both = 2 * count

    @pl.when(step == 0)
    def _():
        high, low = split(left_ref[...].T * (0.5 * step_size / count))
        lefts[:, :both] = high
        lefts[:, both : 2 * both] = high
        lefts[:, 2 * both :] = low

    for at, ref in ((0, proj_ref), (count, samples_ref)):
        high, low = split(ref[...])
        rights[at : at + count, :] = high
        rights[both + at : both + at + count, :] = low
        rights[2 * both + at : 2 * both + at + count, :] = high
    limit = step_size * penalty
    for part in range(parts):
        rows = pl.ds(part * height, height)
        row_at, col_at = offset_ref[0] + part * height, offset_ref[1] + step * tile
        hit = crosses(row_at, col_at, (height, tile))
        cross = dot(lefts[rows, :], rights[...])
        stepped = values_ref[rows, :] * mask_ref[part : part + 1, :] - cross
        out_ref[rows, :] = stepped - jnp.clip(stepped, -limit, limit)

        @pl.when(hit)
        def _(rows=rows, row_at=row_at, col_at=col_at):
            diag = diag_ref[rows, :]
            product = dot(lefts[rows, :], rights[...])
            diagonal = on_diagonal(row_at, col_at, product.shape)
            out_ref[rows, :] = jnp.where(diagonal, diag - product + step_size / diag, out_ref[rows, :])


def reduce_kernel(
    lines, groups, per_group, spans, deeps, samples_ref, values_ref, diag_ref, mask_ref, out_ref, left_ref, *scratch
):
    chunks = spans * deeps
    (core_in, y_in, a_right, a_left, b_right, b_left, y_right, y_left) = scratch[:8]
    send, recv = scratch[8], scratch[9]
    part_ref, held, lefts, rights, held_sem, fetch_send, fetch_sem = scratch[10:]
    row, col = lax.axis_index("row"), lax.axis_index("col")
    core, side, line = row % 2, row // 2 % 2, row // 4
    last = lines - 1
    core_mate = row + 1 - 2 * core
    y_mate = row + 2 - 4 * side
    up, down = row + 4, row - 4
    samples, columns = part_ref.shape
    order = columns // spans
    deep = samples // deeps
    half, quarter, eighth, sixteenth = order // 2, order // 4, order // 8, order // 16
    has_up, has_down = line < last, line > 0
    owner = row // per_group
    width = left_ref.shape[1]
    rows_ref, proj_ref = left_ref.at[:samples, :], left_ref.at[samples:, :]
    slice_at = pl.multiple_of(row % per_group * width, width)

    barrier = pltpu.get_barrier_semaphore()

    def greet(target):
        pl.semaphore_signal(barrier, inc=1, device_id=target, device_id_type=MESH)

    greet((core_mate, col))
    greet((y_mate, col))
    pl.when(has_up)(lambda: greet((up, col)))
    pl.when(has_down)(lambda: greet((down, col)))
    for shift in range(1, groups):
        greet((row, lax.rem(col + shift, groups)))
    ends = jnp.where(has_up, 1, 0) + jnp.where(has_down, 1, 0)
    pl.semaphore_wait(barrier, 2 + groups - 1 + ends)

    def span(at, size):
        return pl.ds(pl.multiple_of(at, sixteenth), size)

    def rows_of(q):
        return pl.ds(pl.multiple_of(q % deeps * deep, deep), deep)

    def base(q):
        return q // deeps * order

    def a_at(q, k, v):
        return base(q) + k * half + v * eighth

    def b_at(q, k):
        return base(q) + k * half + quarter

    def copy(kind, q, source, target, device, landing=None):
        return pltpu.make_async_remote_copy(
            src_ref=source,
            dst_ref=target,
            send_sem=send.at[kind, q],
            recv_sem=recv.at[kind if landing is None else landing, q],
            device_id=device,
            device_id_type=MESH,
        )

    def whole(ref, q):
        return ref.at[q]

    def out_at(q, at, size):
        return out_ref.at[rows_of(q), span(at, size)]

    def c_core(q):
        return copy(0, q, part_ref.at[rows_of(q), span(base(q) + (1 - core) * half, half)], whole(core_in, q), (core_mate, col))

    def c_y(q):
        return copy(1, q, core_in.at[q, :, span((1 - side) * eighth, eighth)], whole(y_in, q), (y_mate, col))

    def c_b_right(q, first):
        source = core_in.at[q, :, span(quarter, eighth)] if first else whole(b_right, q)
        return copy(2, q, source, whole(b_right, q), (up, col))

    def c_b_left(q, first):
        source = core_in.at[q, :, span(quarter + eighth, eighth)] if first else whole(b_left, q)
        return copy(3, q, source, whole(b_left, q), (down, col))

    def c_a_right(q, first):
        source = y_in.at[q, :, span(0, sixteenth)] if first else whole(a_right, q)
        return copy(4, q, source, whole(a_right, q), (up, col))

    def c_a_left(q, first):
        source = y_in.at[q, :, span(sixteenth, sixteenth)] if first else whole(a_left, q)
        return copy(5, q, source, whole(a_left, q), (down, col))

    def c_y_right(q):
        return copy(6, q, whole(b_right, q), whole(y_right, q), (y_mate, col))

    def c_y_left(q):
        return copy(7, q, whole(b_left, q), whole(y_left, q), (y_mate, col))

    def spread(kind, q, at, size, target):
        return copy(kind, q, out_at(q, at, size), out_at(q, at, size), (target, col))

    def b_piece(q, flow):
        return b_at(q, core) + flow * eighth, eighth

    def a_piece(q, flow, v):
        return a_at(q, core, v) + flow * sixteenth, sixteenth

    def c_b_back(q, flow):
        return spread(8 + flow, q, *b_piece(q, flow), (down, up)[flow])

    def c_a_back(q, flow):
        return spread(10 + flow, q, *a_piece(q, flow, side), (down, up)[flow])

    def c_y_back(q, flow):
        return spread(12 + flow, q, *a_piece(q, flow, side), y_mate)

    def y_back_arrival(q, flow):
        return spread(12 + flow, q, *a_piece(q, flow, 1 - side), y_mate)

    def c_core_back(q, index, at, size):
        return copy(14 + index, q, out_at(q, at, size), out_at(q, at, size), (core_mate, col), 14 + index)

    def core_arrival(q, index, at, size):
        other = at - core * half + (1 - core) * half
        return c_core_back(q, index, other, size)

    def pieces(q):
        for flow in range(2):
            yield flow, *b_piece(q, flow)
            yield 2 + flow, *a_piece(q, flow, side)
            yield 4 + flow, *a_piece(q, flow, 1 - side)

    def core_pieces_in(q):
        for index, at, size in pieces(q):
            core_arrival(q, index, at, size).wait_recv()

    def c_proj(q, shift):
        d = q % deeps
        return copy(
            20 + shift,
            d,
            out_ref.at[rows_of(q), pl.ds(slice_at, width)],
            proj_ref.at[rows_of(q), :],
            (row, lax.rem(col + shift, groups)),
            21,
        )

    def at_stage(t, offset, condition, action):
        q = t - offset
        live = jnp.logical_and(q >= 0, q < chunks)
        if condition is not None:
            live = jnp.logical_and(live, condition)
        pl.when(live)(lambda: action(jnp.clip(q, 0, chunks - 1)))

    def begin(q):
        c_core(q).wait_recv()
        rows = rows_of(q)
        core_in[q] = core_in[q] + part_ref[rows, span(base(q) + core * half, half)]
        c_y(q).start()
        pl.when(line == 0)(lambda: c_b_right(q, True).start())
        pl.when(line == last)(lambda: c_b_left(q, True).start())

    def after_y(q):
        c_y(q).wait_recv()
        y_in[q] = y_in[q] + core_in[q, :, span(side * eighth, eighth)]
        pl.when(line == 0)(lambda: c_a_right(q, True).start())
        pl.when(line == last)(lambda: c_a_left(q, True).start())

    def b_hop(q, flow):
        ref, make = (b_right, c_b_right) if flow == 0 else (b_left, c_b_left)
        make(q, False).wait_recv()
        ref[q] = ref[q] + core_in[q, :, span(quarter + flow * eighth, eighth)]
        going = has_up if flow == 0 else has_down
        pl.when(going)(lambda: make(q, False).start())
        pl.when(jnp.logical_not(going))(lambda: (c_y_right if flow == 0 else c_y_left)(q).start())

    def done_a(q, flow, forward):
        pl.when(forward)(lambda: c_a_back(q, flow).start())
        c_y_back(q, flow).start()
        c_core_back(q, 2 + flow, *a_piece(q, flow, side)).start()

    def done_b(q, flow, forward):
        pl.when(forward)(lambda: c_b_back(q, flow).start())
        c_core_back(q, flow, *b_piece(q, flow)).start()

    def a_hop(q, flow):
        ref, make = (a_right, c_a_right) if flow == 0 else (a_left, c_a_left)
        make(q, False).wait_recv()
        rows = rows_of(q)
        value = ref[q] + y_in[q, :, span(flow * sixteenth, sixteenth)]
        going = has_up if flow == 0 else has_down

        @pl.when(going)
        def _():
            ref[q] = value
            make(q, False).start()

        @pl.when(jnp.logical_not(going))
        def _():
            out_ref[rows, span(*a_piece(q, flow, side))] = value
            done_a(q, flow, True)

    def b_end(q, flow):
        ref, other, make = (b_right, y_right, c_y_right) if flow == 0 else (b_left, y_left, c_y_left)
        make(q).wait_recv()
        rows = rows_of(q)
        out_ref[rows, span(*b_piece(q, flow))] = ref[q] + other[q]
        done_b(q, flow, True)

    def back(q, flow):
        forward = has_down if flow == 0 else has_up
        c_a_back(q, flow).wait_recv()
        done_a(q, flow, forward)
        c_b_back(q, flow).wait_recv()
        done_b(q, flow, forward)

    def y_gather(q, flow):
        y_back_arrival(q, flow).wait_recv()
        c_core_back(q, 4 + flow, *a_piece(q, flow, 1 - side)).start()

    def finish(q):
        core_pieces_in(q)
        rows = rows_of(q)

        @pl.when(jnp.logical_and(col == owner, q // deeps == slice_at // order))
        def _():
            for shift in range(1, groups):
                c_proj(q, shift).start()
            proj_ref[rows, :] = out_ref[rows, pl.ds(slice_at, width)]

    height = values_ref.shape[0]
    parts = mask_ref.shape[0]
    block = height // parts
    tile = order // deeps

    def load(i):
        slot = i % 2
        at = pl.multiple_of(i * tile, tile)
        return pltpu.make_async_copy(values_ref.at[:, pl.ds(at, tile)], held.at[slot], held_sem.at[slot])

    load(0).start()
    load(1).start()
    mine = samples_ref.at[:, pl.ds(slice_at, width)]

    def fetch(shift):
        return pltpu.make_async_remote_copy(
            src_ref=mine,
            dst_ref=rows_ref,
            send_sem=fetch_send.at[shift],
            recv_sem=fetch_sem.at[0],
            device_id=(row, lax.rem(col + shift, groups)),
            device_id_type=MESH,
        )

    @pl.when(col == owner)
    def _():
        for shift in range(1, groups):
            fetch(shift).start()
        own = pltpu.make_async_copy(mine, rows_ref, fetch_sem.at[1])
        own.start()
        own.wait()

    @pl.when(col != owner)
    def _():
        fetch(1).wait_recv()

    high, low = split(rows_ref[...])
    lefts[:, :height] = high
    lefts[:, height : 2 * height] = high
    lefts[:, 2 * height :] = low

    def project(i):
        load(i).wait()
        slot = i % 2
        cols = pl.ds(pl.multiple_of(i * tile, tile), tile)
        for index in range(parts):
            begin_at = index * block
            rows = pl.ds(begin_at, block)
            row_at, col_at = row * height + begin_at, col * columns + i * tile
            hit = crosses(row_at, col_at, (block, tile))

            def put(omega, begin_at=begin_at):
                high, low = split(omega)
                rights[begin_at : begin_at + block, :] = high
                rights[height + begin_at : height + begin_at + block, :] = low
                rights[2 * height + begin_at : 2 * height + begin_at + block, :] = high

            masked = held[slot, rows, :] * mask_ref[index : index + 1, cols]
            put(masked)

            @pl.when(hit)
            def _(rows=rows, row_at=row_at, col_at=col_at, put=put, index=index):
                again = held[slot, rows, :] * mask_ref[index : index + 1, cols]
                put(jnp.where(on_diagonal(row_at, col_at, again.shape), diag_ref[rows, :], again))

        part_ref[:, cols] = dot(lefts[...], rights[...])
        pl.when(i + 2 < chunks)(lambda: load(i + 2).start())

        @pl.when(i % deeps == deeps - 1)
        def _():
            for index in range(deeps):
                c_core(i - (deeps - 1) + index).start()

    total = 2 * lines + 2 + deeps

    @pl.loop(0, chunks + total)
    def _(t):
        at_stage(t, 0, None, project)
        at_stage(t - deeps, 0, None, begin)
        at_stage(t - deeps, 1, None, after_y)
        at_stage(t - deeps, line, has_down, lambda q: b_hop(q, 0))
        at_stage(t - deeps, last - line, has_up, lambda q: b_hop(q, 1))
        at_stage(t - deeps, 1 + line, has_down, lambda q: a_hop(q, 0))
        at_stage(t - deeps, lines - line, has_up, lambda q: a_hop(q, 1))
        at_stage(t - deeps, lines, line == last, lambda q: b_end(q, 0))
        at_stage(t - deeps, lines, line == 0, lambda q: b_end(q, 1))
        at_stage(t - deeps, lines + last - line, has_up, lambda q: back(q, 0))
        at_stage(t - deeps, lines + line, has_down, lambda q: back(q, 1))
        at_stage(t - deeps, lines + last - line + 1, None, lambda q: y_gather(q, 0))
        at_stage(t - deeps, lines + line + 1, None, lambda q: y_gather(q, 1))
        at_stage(t - deeps, 2 * lines + 1, None, finish)

    @pl.loop(0, chunks)
    def _(q):
        c_core(q).wait_send()
        c_y(q).wait_send()
        pl.when(has_up)(lambda: c_b_right(q, False).wait_send())
        pl.when(has_down)(lambda: c_b_left(q, False).wait_send())
        pl.when(has_up)(lambda: c_a_right(q, False).wait_send())
        pl.when(has_down)(lambda: c_a_left(q, False).wait_send())
        pl.when(line == last)(lambda: c_y_right(q).wait_send())
        pl.when(line == 0)(lambda: c_y_left(q).wait_send())
        for flow, forward in ((0, has_down), (1, has_up)):
            pl.when(forward)(lambda flow=flow: c_b_back(q, flow).wait_send())
            pl.when(forward)(lambda flow=flow: c_a_back(q, flow).wait_send())
            c_y_back(q, flow).wait_send()
        for index, at, size in pieces(q):
            c_core_back(q, index, at, size).wait_send()

    @pl.when(col == owner)
    def _():
        for shift in range(1, groups):
            fetch(shift).wait_send()

    @pl.loop(0, deeps)
    def _(q):
        @pl.when(col == owner)
        def _():
            for shift in range(1, groups):
                c_proj(q, shift).wait_send()

        @pl.when(col != owner)
        def _():
            c_proj(q, 1).wait_recv()


def per_device(samples, values, diag_entries, block_mask):
    height, order = values.shape
    count = samples.shape[0]
    groups = lax.axis_size("col")
    lines = lax.axis_size("row") // 4
    per_group = order // height
    row_at = lax.axis_index("row") * height
    col_at = lax.axis_index("col") * order
    block = groups * order // block_mask.shape[0]
    tile_mask = lax.dynamic_slice(
        block_mask, (row_at // block, col_at // block), (height // block, order // block)
    )
    mask = jnp.repeat(tile_mask.astype(jnp.float32), block, axis=1)
    diag = diag_entries[:, None]
    offsets = jnp.stack([row_at, col_at]).astype(jnp.int32)
    anywhere = pl.BlockSpec(memory_space=pl.ANY)
    in_vmem = pl.BlockSpec(memory_space=VM)
    parts = mask.shape[0]
    tile = 2 * block
    spans = max(1, order // (16 * 128))
    deeps = order // spans // tile
    chunks = spans * deeps
    deep = count // deeps
    wide = order // spans
    eighth, sixteenth = wide // 8, wide // 16
    widths = [wide // 2, eighth, sixteenth, sixteenth, eighth, eighth, eighth, eighth]
    kinds = 21 + groups
    projected, left = pl.pallas_call(
        functools.partial(reduce_kernel, lines, groups, per_group, spans, deeps),
        out_shape=(
            jax.ShapeDtypeStruct((count, order), jnp.float32),
            jax.ShapeDtypeStruct((2 * count, height), jnp.float32),
        ),
        in_specs=[anywhere, anywhere, in_vmem, in_vmem],
        out_specs=(in_vmem, in_vmem),
        scratch_shapes=[VM((chunks, deep, w), jnp.float32) for w in widths]
        + [pltpu.SemaphoreType.DMA((kinds, chunks)), pltpu.SemaphoreType.DMA((kinds, chunks))]
        + [
            VM((count, order), jnp.float32),
            VM((2, height, tile), jnp.float32),
            VM((count, 3 * height), jnp.bfloat16),
            VM((3 * height, tile), jnp.bfloat16),
            pltpu.SemaphoreType.DMA((2,)),
            pltpu.SemaphoreType.DMA((groups,)),
            pltpu.SemaphoreType.DMA((2,)),
        ],
        compiler_params=pltpu.CompilerParams(
            collective_id=1, has_side_effects=True, vmem_limit_bytes=LIMIT
        ),
    )(samples, values, diag, mask)

    grid = order // tile
    fixed = lambda shape: pl.BlockSpec(shape, lambda i, s: (0, 0))
    moving = lambda rows: pl.BlockSpec((rows, tile), lambda i, s: (0, i))
    return pl.pallas_call(
        update_kernel,
        out_shape=jax.ShapeDtypeStruct((height, order), jnp.float32),
        grid_spec=pltpu.PrefetchScalarGridSpec(
            num_scalar_prefetch=1,
            grid=(grid,),
            in_specs=[
                fixed((2 * count, height)),
                moving(count),
                moving(count),
                moving(height),
                fixed((height, 1)),
                moving(parts),
            ],
            out_specs=moving(height),
            scratch_shapes=[
                VM((height, 6 * count), jnp.bfloat16),
                VM((6 * count, tile), jnp.bfloat16),
            ],
        ),
        compiler_params=pltpu.CompilerParams(dimension_semantics=("arbitrary",), vmem_limit_bytes=LIMIT),
    )(offsets, left, projected, samples, values, diag, mask)


def solution(mesh):
    in_specs = (P(None, "col"), P("row", "col"), P("row"), P())
    out_specs = P("row", "col")
    return jax.shard_map(
        per_device, mesh=mesh, in_specs=in_specs, out_specs=out_specs, check_vma=False
    )
```

```python
import functools

import jax
import jax.numpy as jnp
from jax import lax
from jax.experimental import pallas as pl
from jax.experimental.pallas import tpu as pltpu
from jax.sharding import PartitionSpec as P

step_size = 8.0
penalty = 0.05
MESH = pl.DeviceIdType.MESH
VM = pltpu.VMEM
LIMIT = 60 * 1024 * 1024


def split(x):
    high = x.astype(jnp.bfloat16)
    low = (x - high.astype(jnp.float32)).astype(jnp.bfloat16)
    return high, low


def dot(a, b):
    return jnp.dot(a, b, preferred_element_type=jnp.float32)


def on_diagonal(row_at, col_at, shape):
    rows = lax.broadcasted_iota(jnp.int32, shape, 0) + row_at
    cols = lax.broadcasted_iota(jnp.int32, shape, 1) + col_at
    return rows == cols


def masked(mask_ref, values, row_at, col_at, block):
    pieces = [
        values[:, at : at + block] * mask_ref[row_at // block, (col_at + at) // block].astype(jnp.float32)
        for at in range(0, values.shape[1], block)
    ]
    return jnp.concatenate(pieces, axis=1)


def crosses(row_at, col_at, shape):
    return jnp.logical_and(row_at < col_at + shape[1], col_at < row_at + shape[0])


def update_kernel(left_ref, proj_ref, samples_ref, values_ref, diag_ref, mask_ref, out_ref, lefts, rights):
    step = pl.program_id(0)
    count = samples_ref.shape[0]
    height, tile = values_ref.shape
    both = 2 * count
    block = lax.axis_size("col") * pl.num_programs(0) * tile // mask_ref.shape[0]
    row_at = lax.axis_index("row") * height
    col_at = (lax.axis_index("col") * pl.num_programs(0) + step) * tile

    @pl.when(step == 0)
    def _():
        high, low = split(left_ref[...].T * (0.5 * step_size / count))
        lefts[:, :both] = high
        lefts[:, both:] = low

    for at, ref in ((0, proj_ref), (count, samples_ref)):
        high, low = split(ref[...])
        rights[at : at + count, :] = high
        rights[both + at : both + at + count, :] = low
    limit = step_size * penalty

    def update(hit):
        for begin in range(0, height, block):
            rows = pl.ds(begin, block)
            left_high, left_low = lefts[rows, :both], lefts[rows, both:]
            cross = dot(left_high, rights[:both, :]) + dot(left_low, rights[:both, :]) + dot(left_high, rights[both:, :])
            omega = masked(mask_ref, values_ref[rows, :], row_at + begin, col_at, block)
            stepped = omega - cross
            new = stepped - jnp.clip(stepped, -limit, limit)
            if hit:
                diag = diag_ref[:, pl.ds(pl.multiple_of(col_at - row_at, tile), tile)]
                new = jnp.where(
                    on_diagonal(row_at + begin, col_at, new.shape), diag - cross + step_size / diag, new
                )
            out_ref[rows, :] = new

    hit = crosses(row_at, col_at, (height, tile))
    pl.when(hit)(lambda: update(True))
    pl.when(jnp.logical_not(hit))(lambda: update(False))


def reduce_kernel(
    lines, groups, per_group, spans, deeps, samples_ref, values_ref, diag_ref, mask_ref, out_ref, left_ref, *scratch
):
    chunks = spans * deeps
    (core_in, y_in, a_right, a_left, b_right, b_left, y_right, y_left) = scratch[:8]
    send, recv = scratch[8], scratch[9]
    part_ref, held, lefts, rights, held_sem, fetch_send, fetch_sem = scratch[10:]
    row, col = lax.axis_index("row"), lax.axis_index("col")
    core, side, line = row % 2, row // 2 % 2, row // 4
    last = lines - 1
    core_mate = row + 1 - 2 * core
    y_mate = row + 2 - 4 * side
    up, down = row + 4, row - 4
    samples, columns = part_ref.shape
    order = columns // spans
    deep = samples // deeps
    half, quarter, eighth, sixteenth = order // 2, order // 4, order // 8, order // 16
    has_up, has_down = line < last, line > 0
    owner = row // per_group
    width = left_ref.shape[1]
    rows_ref, proj_ref = left_ref.at[:samples, :], left_ref.at[samples:, :]
    slice_at = pl.multiple_of(row % per_group * width, width)

    barrier = pltpu.get_barrier_semaphore()

    def greet(target):
        pl.semaphore_signal(barrier, inc=1, device_id=target, device_id_type=MESH)

    greet((core_mate, col))
    greet((y_mate, col))
    pl.when(has_up)(lambda: greet((up, col)))
    pl.when(has_down)(lambda: greet((down, col)))
    for shift in range(1, groups):
        greet((row, lax.rem(col + shift, groups)))
    ends = jnp.where(has_up, 1, 0) + jnp.where(has_down, 1, 0)
    pl.semaphore_wait(barrier, 2 + groups - 1 + ends)

    def span(at, size):
        return pl.ds(pl.multiple_of(at, sixteenth), size)

    def rows_of(q):
        return pl.ds(pl.multiple_of(q % deeps * deep, deep), deep)

    def base(q):
        return q // deeps * order

    def a_at(q, k, v):
        return base(q) + k * half + v * eighth

    def b_at(q, k):
        return base(q) + k * half + quarter

    def copy(kind, q, source, target, device, landing=None):
        return pltpu.make_async_remote_copy(
            src_ref=source,
            dst_ref=target,
            send_sem=send.at[kind, q],
            recv_sem=recv.at[kind if landing is None else landing, q],
            device_id=device,
            device_id_type=MESH,
        )

    def whole(ref, q):
        return ref.at[q]

    def out_at(q, at, size):
        return out_ref.at[rows_of(q), span(at, size)]

    def c_core(q):
        return copy(0, q, part_ref.at[rows_of(q), span(base(q) + (1 - core) * half, half)], whole(core_in, q), (core_mate, col))

    def c_y(q):
        return copy(1, q, core_in.at[q, :, span((1 - side) * eighth, eighth)], whole(y_in, q), (y_mate, col))

    def c_b_right(q, first):
        source = core_in.at[q, :, span(quarter, eighth)] if first else whole(b_right, q)
        return copy(2, q, source, whole(b_right, q), (up, col))

    def c_b_left(q, first):
        source = core_in.at[q, :, span(quarter + eighth, eighth)] if first else whole(b_left, q)
        return copy(3, q, source, whole(b_left, q), (down, col))

    def c_a_right(q, first):
        source = y_in.at[q, :, span(0, sixteenth)] if first else whole(a_right, q)
        return copy(4, q, source, whole(a_right, q), (up, col))

    def c_a_left(q, first):
        source = y_in.at[q, :, span(sixteenth, sixteenth)] if first else whole(a_left, q)
        return copy(5, q, source, whole(a_left, q), (down, col))

    def c_y_right(q):
        return copy(6, q, whole(b_right, q), whole(y_right, q), (y_mate, col))

    def c_y_left(q):
        return copy(7, q, whole(b_left, q), whole(y_left, q), (y_mate, col))

    def spread(kind, q, at, size, target):
        return copy(kind, q, out_at(q, at, size), out_at(q, at, size), (target, col))

    def b_piece(q, flow):
        return b_at(q, core) + flow * eighth, eighth

    def a_piece(q, flow, v):
        return a_at(q, core, v) + flow * sixteenth, sixteenth

    def c_b_back(q, flow):
        return spread(8 + flow, q, *b_piece(q, flow), (down, up)[flow])

    def c_a_back(q, flow):
        return spread(10 + flow, q, *a_piece(q, flow, side), (down, up)[flow])

    def c_y_back(q, flow):
        return spread(12 + flow, q, *a_piece(q, flow, side), y_mate)

    def y_back_arrival(q, flow):
        return spread(12 + flow, q, *a_piece(q, flow, 1 - side), y_mate)

    def c_core_back(q, index, at, size):
        return copy(14 + index, q, out_at(q, at, size), out_at(q, at, size), (core_mate, col), 14 + index)

    def core_arrival(q, index, at, size):
        other = at - core * half + (1 - core) * half
        return c_core_back(q, index, other, size)

    def pieces(q):
        for flow in range(2):
            yield flow, *b_piece(q, flow)
            yield 2 + flow, *a_piece(q, flow, side)
            yield 4 + flow, *a_piece(q, flow, 1 - side)

    def core_pieces_in(q):
        for index, at, size in pieces(q):
            core_arrival(q, index, at, size).wait_recv()

    def c_proj(q, shift):
        d = q % deeps
        return copy(
            20 + shift,
            d,
            out_ref.at[rows_of(q), pl.ds(slice_at, width)],
            proj_ref.at[rows_of(q), :],
            (row, lax.rem(col + shift, groups)),
            21,
        )

    def at_stage(t, offset, condition, action):
        q = t - offset
        live = jnp.logical_and(q >= 0, q < chunks)
        if condition is not None:
            live = jnp.logical_and(live, condition)
        pl.when(live)(lambda: action(jnp.clip(q, 0, chunks - 1)))

    def begin(q):
        c_core(q).wait_recv()
        rows = rows_of(q)
        core_in[q] = core_in[q] + part_ref[rows, span(base(q) + core * half, half)]
        c_y(q).start()
        pl.when(line == 0)(lambda: c_b_right(q, True).start())
        pl.when(line == last)(lambda: c_b_left(q, True).start())

    def after_y(q):
        c_y(q).wait_recv()
        y_in[q] = y_in[q] + core_in[q, :, span(side * eighth, eighth)]
        pl.when(line == 0)(lambda: c_a_right(q, True).start())
        pl.when(line == last)(lambda: c_a_left(q, True).start())

    def b_hop(q, flow):
        ref, make = (b_right, c_b_right) if flow == 0 else (b_left, c_b_left)
        make(q, False).wait_recv()
        ref[q] = ref[q] + core_in[q, :, span(quarter + flow * eighth, eighth)]
        going = has_up if flow == 0 else has_down
        pl.when(going)(lambda: make(q, False).start())
        pl.when(jnp.logical_not(going))(lambda: (c_y_right if flow == 0 else c_y_left)(q).start())

    def done_a(q, flow, forward):
        pl.when(forward)(lambda: c_a_back(q, flow).start())
        c_y_back(q, flow).start()
        c_core_back(q, 2 + flow, *a_piece(q, flow, side)).start()

    def done_b(q, flow, forward):
        pl.when(forward)(lambda: c_b_back(q, flow).start())
        c_core_back(q, flow, *b_piece(q, flow)).start()

    def a_hop(q, flow):
        ref, make = (a_right, c_a_right) if flow == 0 else (a_left, c_a_left)
        make(q, False).wait_recv()
        rows = rows_of(q)
        value = ref[q] + y_in[q, :, span(flow * sixteenth, sixteenth)]
        going = has_up if flow == 0 else has_down

        @pl.when(going)
        def _():
            ref[q] = value
            make(q, False).start()

        @pl.when(jnp.logical_not(going))
        def _():
            out_ref[rows, span(*a_piece(q, flow, side))] = value
            done_a(q, flow, True)

    def b_end(q, flow):
        ref, other, make = (b_right, y_right, c_y_right) if flow == 0 else (b_left, y_left, c_y_left)
        make(q).wait_recv()
        rows = rows_of(q)
        out_ref[rows, span(*b_piece(q, flow))] = ref[q] + other[q]
        done_b(q, flow, True)

    def back(q, flow):
        forward = has_down if flow == 0 else has_up
        c_a_back(q, flow).wait_recv()
        done_a(q, flow, forward)
        c_b_back(q, flow).wait_recv()
        done_b(q, flow, forward)

    def y_gather(q, flow):
        y_back_arrival(q, flow).wait_recv()
        c_core_back(q, 4 + flow, *a_piece(q, flow, 1 - side)).start()

    def finish(q):
        core_pieces_in(q)
        rows = rows_of(q)

        @pl.when(jnp.logical_and(col == owner, q // deeps == slice_at // order))
        def _():
            for shift in range(1, groups):
                c_proj(q, shift).start()
            proj_ref[rows, :] = out_ref[rows, pl.ds(slice_at, width)]

    height = values_ref.shape[0]
    block = groups * columns // mask_ref.shape[0]
    tile = order // deeps

    def load(i):
        slot = i % 2
        at = pl.multiple_of(i * tile, tile)
        return pltpu.make_async_copy(values_ref.at[:, pl.ds(at, tile)], held.at[slot], held_sem.at[slot])

    load(0).start()
    load(1).start()
    mine = samples_ref.at[:, pl.ds(slice_at, width)]

    def fetch(shift):
        return pltpu.make_async_remote_copy(
            src_ref=mine,
            dst_ref=rows_ref,
            send_sem=fetch_send.at[shift],
            recv_sem=fetch_sem.at[0],
            device_id=(row, lax.rem(col + shift, groups)),
            device_id_type=MESH,
        )

    @pl.when(col == owner)
    def _():
        for shift in range(1, groups):
            fetch(shift).start()
        own = pltpu.make_async_copy(mine, rows_ref, fetch_sem.at[1])
        own.start()
        own.wait()

    @pl.when(col != owner)
    def _():
        fetch(1).wait_recv()

    high, low = split(rows_ref[...])
    lefts[:, :height] = high
    lefts[:, height : 2 * height] = high
    lefts[:, 2 * height :] = low

    def project(i):
        load(i).wait()
        slot = i % 2
        cols = pl.ds(pl.multiple_of(i * tile, tile), tile)
        row_at, col_at = row * height, col * columns + i * tile
        hit = crosses(row_at, col_at, (height, tile))

        def put(hit):
            for begin_at in range(0, height, block):
                omega = masked(mask_ref, held[slot, pl.ds(begin_at, block), :], row_at + begin_at, col_at, block)
                if hit:
                    diag = diag_ref[:, pl.ds(pl.multiple_of(col_at - row_at, tile), tile)]
                    omega = jnp.where(on_diagonal(row_at + begin_at, col_at, omega.shape), diag, omega)
                high, low = split(omega)
                rights[begin_at : begin_at + block, :] = high
                rights[height + begin_at : height + begin_at + block, :] = low

        pl.when(hit)(lambda: put(True))
        pl.when(jnp.logical_not(hit))(lambda: put(False))
        part_ref[:, cols] = dot(lefts[:, : 2 * height], rights[...]) + dot(lefts[:, 2 * height :], rights[:height, :])
        pl.when(i + 2 < chunks)(lambda: load(i + 2).start())

        @pl.when(i % deeps == deeps - 1)
        def _():
            for index in range(deeps):
                c_core(i - (deeps - 1) + index).start()

    total = 2 * lines + 2 + deeps

    @pl.loop(0, chunks + total)
    def _(t):
        at_stage(t, 0, None, project)
        at_stage(t - deeps, 0, None, begin)
        at_stage(t - deeps, 1, None, after_y)
        at_stage(t - deeps, line, has_down, lambda q: b_hop(q, 0))
        at_stage(t - deeps, last - line, has_up, lambda q: b_hop(q, 1))
        at_stage(t - deeps, 1 + line, has_down, lambda q: a_hop(q, 0))
        at_stage(t - deeps, lines - line, has_up, lambda q: a_hop(q, 1))
        at_stage(t - deeps, lines, line == last, lambda q: b_end(q, 0))
        at_stage(t - deeps, lines, line == 0, lambda q: b_end(q, 1))
        at_stage(t - deeps, lines + last - line, has_up, lambda q: back(q, 0))
        at_stage(t - deeps, lines + line, has_down, lambda q: back(q, 1))
        at_stage(t - deeps, lines + last - line + 1, None, lambda q: y_gather(q, 0))
        at_stage(t - deeps, lines + line + 1, None, lambda q: y_gather(q, 1))
        at_stage(t - deeps, 2 * lines + 1, None, finish)

    @pl.loop(0, chunks)
    def _(q):
        c_core(q).wait_send()
        c_y(q).wait_send()
        pl.when(has_up)(lambda: c_b_right(q, False).wait_send())
        pl.when(has_down)(lambda: c_b_left(q, False).wait_send())
        pl.when(has_up)(lambda: c_a_right(q, False).wait_send())
        pl.when(has_down)(lambda: c_a_left(q, False).wait_send())
        pl.when(line == last)(lambda: c_y_right(q).wait_send())
        pl.when(line == 0)(lambda: c_y_left(q).wait_send())
        for flow, forward in ((0, has_down), (1, has_up)):
            pl.when(forward)(lambda flow=flow: c_b_back(q, flow).wait_send())
            pl.when(forward)(lambda flow=flow: c_a_back(q, flow).wait_send())
            c_y_back(q, flow).wait_send()
        for index, at, size in pieces(q):
            c_core_back(q, index, at, size).wait_send()

    @pl.when(col == owner)
    def _():
        for shift in range(1, groups):
            fetch(shift).wait_send()

    @pl.loop(0, deeps)
    def _(q):
        @pl.when(col == owner)
        def _():
            for shift in range(1, groups):
                c_proj(q, shift).wait_send()

        @pl.when(col != owner)
        def _():
            c_proj(q, 1).wait_recv()


def per_device(samples, values, diag_entries, block_mask):
    height, order = values.shape
    count = samples.shape[0]
    groups = lax.axis_size("col")
    lines = lax.axis_size("row") // 4
    per_group = order // height
    block = groups * order // block_mask.shape[0]
    diag = diag_entries[None, :]
    anywhere = pl.BlockSpec(memory_space=pl.ANY)
    in_smem = pl.BlockSpec(memory_space=pltpu.SMEM)
    in_vmem = pl.BlockSpec(memory_space=VM)
    tile = 2 * block
    spans = max(1, order // (16 * 128))
    deeps = order // spans // tile
    chunks = spans * deeps
    deep = count // deeps
    wide = order // spans
    eighth, sixteenth = wide // 8, wide // 16
    widths = [wide // 2, eighth, sixteenth, sixteenth, eighth, eighth, eighth, eighth]
    kinds = 21 + groups
    projected, left = pl.pallas_call(
        functools.partial(reduce_kernel, lines, groups, per_group, spans, deeps),
        out_shape=(
            jax.ShapeDtypeStruct((count, order), jnp.float32),
            jax.ShapeDtypeStruct((2 * count, height), jnp.float32),
        ),
        in_specs=[anywhere, anywhere, in_vmem, in_smem],
        out_specs=(in_vmem, in_vmem),
        scratch_shapes=[VM((chunks, deep, w), jnp.float32) for w in widths]
        + [pltpu.SemaphoreType.DMA((kinds, chunks)), pltpu.SemaphoreType.DMA((kinds, chunks))]
        + [
            VM((count, order), jnp.float32),
            VM((2, height, tile), jnp.float32),
            VM((count, 3 * height), jnp.bfloat16),
            VM((2 * height, tile), jnp.bfloat16),
            pltpu.SemaphoreType.DMA((2,)),
            pltpu.SemaphoreType.DMA((groups,)),
            pltpu.SemaphoreType.DMA((2,)),
        ],
        compiler_params=pltpu.CompilerParams(
            collective_id=1, has_side_effects=True, vmem_limit_bytes=LIMIT
        ),
    )(samples, values, diag, block_mask)

    tile = min(4 * block, height)
    grid = order // tile
    fixed = lambda shape: pl.BlockSpec(shape, lambda i: (0, 0))
    moving = lambda rows: pl.BlockSpec((rows, tile), lambda i: (0, i))
    return pl.pallas_call(
        update_kernel,
        out_shape=jax.ShapeDtypeStruct((height, order), jnp.float32),
        grid=(grid,),
        in_specs=[
            fixed((2 * count, height)),
            moving(count),
            moving(count),
            moving(height),
            fixed((1, height)),
            in_smem,
        ],
        out_specs=moving(height),
        scratch_shapes=[
            VM((height, 4 * count), jnp.bfloat16),
            VM((4 * count, tile), jnp.bfloat16),
        ],
        compiler_params=pltpu.CompilerParams(dimension_semantics=("arbitrary",), vmem_limit_bytes=LIMIT),
    )(left, projected, samples, values, diag, block_mask)


def solution(mesh):
    in_specs = (P(None, "col"), P("row", "col"), P("row"), P())
    out_specs = P("row", "col")
    return jax.shard_map(
        per_device, mesh=mesh, in_specs=in_specs, out_specs=out_specs, check_vma=False
    )
```
